32 devices in a mesh: grp: 4 (over y, x), dev: 8 (over z, core).
Axes of the slice: x: 2, y: 2, z: 4, core: 2. Of those that a mesh axis runs over, the one named last changes fastest.
Arguments:
- face_owner: int32 [131072, 1], P(('grp', 'dev')), may hold values from 0 to 31; in each aligned block of 4096 rows (0 to 4095, 4096 to 8191, ...) at most 256 rows name the same one
- face_element: int32 [131072], P(('grp', 'dev')), may hold values from 0 to 16383
- element_state: bfloat16 [110, 131072], P(None, ('grp', 'dev')), may hold values from -6 to 6
- lift: bfloat16 [30, 110], replicated, may hold values from -0.5 to 0.5
- face_scale: float32 [131072], P(('grp', 'dev')), may hold values from 0.5 to 2
- transfer: float32 [4, 10], replicated, may hold values from 0.05 to 0.5
- stiffness_ref: float32 [12, 12], replicated, may hold values from -0.18 to 5, as said below
- element_scale: float32 [256, 2048], P('grp', 'dev'), may hold values from 1 to 1.1
- displacement_prev: float32 [4, 3, 256, 2048], P(None, None, 'grp', 'dev'), may hold values from -6 to 6
Outputs:
- shell_displacement: float32 [4, 3, 256, 2048], P(None, None, 'grp', 'dev')
- face_displacement: float32 [3, 10, 131072], P(None, None, ('grp', 'dev'))
The draws below stay inside these ranges and needn't reach their ends.
Inputs may be any that keep to these rules, and one draw needn't show every extreme that they name: `face_owner`: among the 4096 faces of one device (aligned blocks), at most 256 name the same owner, and in every draw some device has exactly 256 faces on one owner. `stiffness_ref`: every diagonal entry is 5 and the off-diagonal entries of each row have absolute values summing to at most 2.
All inputs are finite; a program needn't handle non-finite values.
Results may differ from the reference program's by a relative error of at most 0.0003.
Values sent between devices are 32-bit elements; how exact they have to be, the bound alone decides.
A program may use at most 128 MiB of HBM per device.

```python
import math
import jax
import jax.numpy as jnp
import numpy as np
from jax import lax

NODES_F = 10
STATE = 110
SWEEPS = 8
FACES_DEV = 4096
SX = 64
SY = 256
CAP = 256
FACES = 131072
N_GRP = 4
N_DEV = 8
DEVICES = 32


def draw_stiffness_ref(key, part):
    key_one = jax.random.fold_in(jax.random.fold_in(key, 7), 0)
    spread = jax.random.uniform(key_one, (12, 12), jnp.float32, -0.18, 0.18)
    identity = jnp.eye(12, dtype=jnp.float32)
    return spread * (1.0 - identity) + 5.0 * identity


def set_ends(result, rng, low, high):
    shape = result.shape
    place = [jax.random.randint(jax.random.fold_in(rng, axis), (), 0, shape[axis]) for axis in range(len(shape))]
    result = result.at[tuple(place)].set(low)
    longest = shape.index(max(shape))
    place[longest] = (place[longest] + 1) % shape[longest]
    return result.at[tuple(place)].set(high)


def block_scale(rng, dims, shards, low, top_value):
    def one(position, blocks):
        draws = jax.random.uniform(jax.random.fold_in(jax.random.fold_in(rng, 6), position), (blocks,), jnp.float32, low / len(shards), top_value / len(shards))
        return jnp.repeat(jnp.exp(draws), dims[position] // blocks).reshape((-1,) + (1,) * (len(dims) - position - 1))

    factor_of = one(*shards[0])
    for cut in shards[1:]:
        factor_of = factor_of * one(*cut)
    return factor_of


def assign_block(rng, own, number, rows, number_of, top, reach, skew):
    sequence = jax.random.permutation(rng, number_of)
    packed, ordinary = shares(number_of, rows * top, reach, skew, True), shares(number_of, rows * top, reach, skew, False)
    places = jnp.arange(number_of)

    def named(sizes, turn):
        used = int((sizes > 0).sum())
        fixed = max(1, used // 4)
        moved = fixed + (places - fixed + turn * (used - fixed)) % max(1, number_of - fixed)
        return jnp.zeros((number_of,), jnp.int32).at[sequence[jnp.where(places < fixed, places, moved)]].set(jnp.asarray(sizes, jnp.int32))

    sizes = jnp.where(number % 4 == 0, named(packed, number // 4), named(ordinary, number - number // 4 - 1))
    mixed = jax.random.permutation(jax.random.fold_in(own, 3), number_of)
    giver, receiver = mixed[0:number_of // 2 * 2:2], mixed[1:number_of // 2 * 2:2]
    slack = jnp.minimum(sizes[giver] - 1, reach - sizes[receiver]) // 2
    slack = jnp.where((giver == sequence[0]) | (receiver == sequence[0]) | (sizes[receiver] == 0), 0, jnp.maximum(slack, 0))
    moved = jax.random.randint(jax.random.fold_in(own, 4), (number_of // 2,), 0, 1 << 20) % (slack + 1)
    sizes = sizes.at[giver].add(-moved).at[receiver].add(moved)
    labels = jnp.searchsorted(jnp.cumsum(sizes), jnp.arange(rows * top), side="right").astype(jnp.int32)
    listing = labels.reshape(top, rows).T
    listing = listing[jax.random.permutation(jax.random.fold_in(own, 1), rows)]
    turn = jax.random.randint(jax.random.fold_in(own, 2), (rows, 1), 0, top)
    return jnp.take_along_axis(listing, (jnp.arange(top)[None, :] + turn) % top, axis=1)


def shares(number_of, total, limit, skew, full):
    weights = [(1 << 20) // math.isqrt(rank ** skew) + 1 for rank in range(1, number_of + 1)]
    largest = limit if full else min(limit, max(-(-total // number_of), total * weights[0] // sum(weights)))
    least = 1 if total - largest >= number_of - 1 else 0
    given, spare = [largest] + [least] * (number_of - 1), total - largest - least * (number_of - 1)
    while spare > 0:
        free = [i for i in range(1, number_of) if given[i] < largest] or [i for i in range(1, number_of) if given[i] < limit]
        mass, budget = sum([weights[i] for i in free]), spare
        for i in free:
            extra = min(limit - given[i], max(1, budget * weights[i] // mass), spare)
            given[i] = given[i] + extra
            spare = spare - extra
    return np.array(given)


def normal_values(rng, shape, width, most, cuts=(), kind=jnp.bfloat16):
    entries = width * jax.random.normal(rng, shape, jnp.float32)
    if cuts:
        entries = entries * block_scale(rng, shape, cuts, -0.22, 0.18)
    return jnp.clip(entries, -most, most).astype(kind)


def setup_inputs(seed: int = 0) -> dict:
    key_of = jax.random.split(jax.random.key(seed), 10)
    face_owner_keys = jax.random.split(jax.random.fold_in(key_of[0], 1), FACES // FACES_DEV)
    face_owner_turns = jax.random.permutation(jax.random.fold_in(key_of[0], 3), FACES // FACES_DEV)
    face_owner = jax.vmap(lambda own, number: assign_block(jax.random.fold_in(key_of[0], 2), own, number, FACES_DEV, DEVICES, 1, CAP, 1))(face_owner_keys, face_owner_turns).reshape((FACES, 1))
    face_element = set_ends(jax.random.randint(key_of[1], (FACES,), 0, SX * SY), jax.random.fold_in(key_of[1], 1), 0, (SX * SY) - 1).astype(jnp.int32)
    element_state = normal_values(key_of[2], (STATE, FACES), 1.0, 6.0, ((1, 32),))
    lift = normal_values(key_of[3], (3 * NODES_F, STATE), STATE ** -0.5, 0.5)
    face_scale = jnp.clip(jnp.exp(math.log(2.0) - 1.3862944 * jax.random.uniform(key_of[4], (FACES,), jnp.float32) ** block_scale(key_of[4], (FACES,), ((0, 32),), -0.2, 0.2)), 0.5, 2.0)
    transfer = jnp.clip(jax.random.uniform(key_of[5], (4, NODES_F), jnp.float32, 0.05, 0.5), 0.05, 0.5)
    stiffness_ref = draw_stiffness_ref(jax.random.fold_in(key_of[9], 71), 0)
    element_scale = jnp.clip(jnp.exp(math.log(1.1) - 0.095310201 * jax.random.uniform(key_of[7], (SX * N_GRP, SY * N_DEV), jnp.float32) ** block_scale(key_of[7], (SX * N_GRP, SY * N_DEV), ((0, 4), (1, 8)), -0.2, 0.2)), 1.0, 1.1)
    displacement_prev = normal_values(key_of[8], (4, 3, SX * N_GRP, SY * N_DEV), 1.0, 6.0, ((2, 4), (3, 8)), jnp.float32)
    return dict(face_owner=face_owner, face_element=face_element, element_state=element_state, lift=lift, face_scale=face_scale, transfer=transfer, stiffness_ref=stiffness_ref, element_scale=element_scale, displacement_prev=displacement_prev)


coupling_weight = 2.2
highest = lax.Precision.HIGHEST


def invert_block(stiffness_ref):
    identity = jnp.eye(12, dtype=jnp.float32)
    approx = identity / 5.0
    for turn_index in range(8):
        product = jnp.dot(stiffness_ref, approx, precision=highest, preferred_element_type=jnp.float32)
        approx = jnp.dot(approx, 2.0 * identity - product, precision=highest, preferred_element_type=jnp.float32)
    return approx


def couple(padded):
    east_side = padded[:, :, 1:-1, 2:]
    west_side = padded[:, :, 1:-1, :-2]
    north_side = padded[:, :, 2:, 1:-1]
    south_side = padded[:, :, :-2, 1:-1]
    return jnp.stack([west_side[1] + south_side[2], east_side[0] + south_side[3],
                      west_side[3] + north_side[0], east_side[2] + north_side[1]])


def jacobi_sweep(displacement, padded, shell_load, block_inverse, element_scale):
    right_side = shell_load + coupling_weight * couple(padded)
    solved = jnp.dot(block_inverse, right_side.reshape(12, -1), precision=highest, preferred_element_type=jnp.float32)
    return solved.reshape(displacement.shape) / element_scale


def reference(face_owner, face_element, element_state, lift, face_scale, transfer, stiffness_ref, element_scale, displacement_prev):
    traces = jnp.dot(lift, element_state, preferred_element_type=jnp.float32) * face_scale[None, :]
    traction = traces.reshape(3, NODES_F, -1)
    face_load = jnp.einsum("nk,ckf->ncf", transfer, traction, precision=highest).reshape(12, -1)
    owners = face_owner[:, 0]
    grid_width = SY * N_DEV
    grid_row = (owners // N_DEV) * SX + face_element // SY
    grid_col = (owners % N_DEV) * SY + face_element % SY
    target = (grid_row * grid_width + grid_col).astype(jnp.int32)
    shell_load = jnp.zeros((12, SX * N_GRP * grid_width), jnp.float32).at[:, target].add(face_load)
    shell_load = shell_load.reshape(4, 3, SX * N_GRP, grid_width)
    block_inverse = invert_block(stiffness_ref)
    displacement = displacement_prev
    for turn_index in range(SWEEPS):
        padded = jnp.pad(displacement, ((0, 0), (0, 0), (1, 1), (1, 1)))
        displacement = jacobi_sweep(displacement, padded, shell_load, block_inverse, element_scale)
    node_disp = displacement.reshape(12, -1)[:, target].reshape(4, 3, -1)
    face_displacement = jnp.einsum("nk,ncf->ckf", transfer, node_disp, precision=highest)
    return displacement, face_displacement
```

```python
import functools

import jax
import jax.numpy as jnp
from jax import lax
from jax.experimental import pallas as pl
from jax.experimental.pallas import tpu as pltpu
from jax.sharding import PartitionSpec as P

NODES_F = 10
SWEEPS = 8
LANES = 128

coupling_weight = 2.2
highest = lax.Precision.HIGHEST
F32 = jnp.float32
BF16 = jnp.bfloat16
NT = (((1,), (1,)), ((), ()))
VM = pl.BlockSpec(memory_space=pltpu.VMEM)
SM = pl.BlockSpec(memory_space=pltpu.SMEM)


def split(x):
    high = x.astype(BF16).astype(F32)
    return high, x - high


def one_hot(row, count):
    places = lax.broadcasted_iota(jnp.int32, (count, row.shape[1]), 0).astype(F32)
    return jnp.where(places == row, 1.0, 0.0).astype(BF16)


def route_kernel(n, cap, cols, owner_ref, element_ref, state_ref, lift_ref, scale_ref, spread_ref,
                 stiff_ref, out_ref, rank_ref, inverse_ref, counts):
    step = pl.program_id(0)
    width = owner_ref.shape[1]

    @pl.when(step == 0)
    def _():
        out_ref[...] = jnp.zeros_like(out_ref)
        counts[...] = jnp.zeros_like(counts)
        stiffness = stiff_ref[...]
        identity = (
            lax.broadcasted_iota(jnp.int32, (12, 12), 0)
            == lax.broadcasted_iota(jnp.int32, (12, 12), 1)
        ).astype(F32)
        approx = identity / 5.0
        for _ in range(8):
            product = jnp.dot(stiffness, approx, precision=highest, preferred_element_type=F32)
            approx = jnp.dot(
                approx, 2.0 * identity - product, precision=highest, preferred_element_type=F32
            )
        inverse_ref[...] = approx

    owner = owner_ref[...]
    owner_f = owner.astype(F32)
    traces = jnp.dot(lift_ref[...], state_ref[...], preferred_element_type=F32) * scale_ref[...]
    loads = jnp.dot(spread_ref[...], traces, precision=highest, preferred_element_type=F32)
    element = element_ref[...]
    high_row = (element // cols).astype(F32)
    low_row = (element % cols).astype(F32)
    where_row = lax.broadcasted_iota(jnp.int32, loads.shape, 0)
    values = jnp.where(where_row == 12, high_row, jnp.where(where_row == 13, low_row, loads))

    owner_hot = one_hot(owner_f, n)
    before = (
        lax.broadcasted_iota(jnp.int32, (width, width), 0)
        < lax.broadcasted_iota(jnp.int32, (width, width), 1)
    ).astype(F32).astype(BF16)
    running = jnp.dot(owner_hot, before, preferred_element_type=F32) + counts[:, :1]
    hot = owner_hot.astype(F32)
    rank = jnp.sum(hot * running, axis=0, keepdims=True)
    rank_ref[...] = rank
    counts[...] = counts[...] + jnp.sum(hot, axis=1, keepdims=True)

    slot_hot = one_hot(rank, cap)
    high, low = split(values)
    owner_wide = jnp.broadcast_to(owner, values.shape)
    highs, lows = [], []
    for d in range(n):
        mine = owner_wide == d
        highs.append(jnp.where(mine, high, 0.0).astype(BF16))
        lows.append(jnp.where(mine, low, 0.0).astype(BF16))
    left = jnp.concatenate(
        [jnp.concatenate(highs, axis=0), jnp.concatenate(lows, axis=0)], axis=1
    )
    right = jnp.concatenate([slot_hot, slot_hot], axis=1)
    out_ref[...] += lax.dot_general(left, right, NT, preferred_element_type=F32)


def route(n, cap, cols, owner, element, state, lift, scale, spread, stiffness):
    faces = owner.shape[1]
    width = 512
    whole = lambda a: pl.BlockSpec(a.shape, lambda i: (0,) * a.ndim)
    row = pl.BlockSpec((1, width), lambda i: (0, i))
    return pl.pallas_call(
        functools.partial(route_kernel, n, cap, cols),
        grid=(faces // width,),
        in_specs=[row, row, pl.BlockSpec((state.shape[0], width), lambda i: (0, i)), whole(lift),
                  row, whole(spread), whole(stiffness)],
        out_specs=[pl.BlockSpec((n * 16, cap), lambda i: (0, 0)), row,
                   pl.BlockSpec((12, 12), lambda i: (0, 0))],
        out_shape=[jax.ShapeDtypeStruct((n * 16, cap), F32),
                   jax.ShapeDtypeStruct((1, faces), F32),
                   jax.ShapeDtypeStruct((12, 12), F32)],
        scratch_shapes=[pltpu.VMEM((n, LANES), F32)],
        name="route",
    )(owner, element, state, lift, scale, spread, stiffness)


def lanes_of(ref):
    return jnp.concatenate([ref[g] for g in range(ref.shape[0])], axis=1)


def gather_kernel_in(rows, cols, recv_ref, prev_ref, scale_ref, load_ref, edge_ref, strip_ref):
    step = pl.program_id(0)

    @pl.when(step == 0)
    def _():
        load_ref[...] = jnp.zeros_like(load_ref)

    values = lanes_of(recv_ref)
    width = values.shape[1]
    mask = lax.broadcasted_iota(jnp.int32, (rows, width), 0).astype(F32) == values[12:13]
    low_hot = one_hot(values[13:14], cols)
    high, low = split(values)
    highs, lows = [], []
    for c in range(12):
        highs.append(jnp.where(mask, high[c : c + 1], 0.0).astype(BF16))
        lows.append(jnp.where(mask, low[c : c + 1], 0.0).astype(BF16))
    left = jnp.concatenate(
        [jnp.concatenate(highs, axis=0), jnp.concatenate(lows, axis=0)], axis=1
    )
    right = jnp.concatenate([low_hot, low_hot], axis=1)
    total = lax.dot_general(left, right, NT, preferred_element_type=F32)
    load_ref[...] += total.reshape(12, rows, cols)

    @pl.when(step == pl.num_programs(0) - 1)
    def _():
        scale = scale_ref[...]
        for side, start in ((0, 0), (1, rows - SWEEPS)):
            edge_ref[side, :12] = prev_ref[:, start : start + SWEEPS, :]
            edge_ref[side, 12] = scale[start : start + SWEEPS]
            edge_ref[side, 13:] = load_ref[:, start : start + SWEEPS, :]
        lane = lax.broadcasted_iota(jnp.int32, (rows, LANES), 1) // SWEEPS
        for side in range(2):
            base = 0 if side == 0 else cols - LANES
            turn = 0 if side == 0 else SWEEPS
            for kind in range(2):
                pieces = [(prev_ref if kind == 0 else load_ref)[c, :, base : base + LANES] for c in range(12)]
                if kind == 0:
                    pieces.append(scale[:, base : base + LANES])
                packed = jnp.zeros((rows, LANES), F32)
                for j, piece in enumerate(pieces):
                    move = (j * SWEEPS + turn) % LANES
                    piece = pltpu.roll(piece, move, 1) if move else piece
                    packed = jnp.where(lane == j, piece, packed)
                strip_ref[side, kind] = packed


def collect(rows, cols, recv, prev, scale):
    groups, _, cap = recv.shape
    block = max(1, min(groups, 1024 // cap))
    whole = lambda shape: pl.BlockSpec(shape, lambda i: (0,) * len(shape))
    shapes = [(12, rows, cols), (2, 25, SWEEPS, cols), (2, 2, rows, LANES)]
    return pl.pallas_call(
        functools.partial(gather_kernel_in, rows, cols),
        grid=(groups // block,),
        in_specs=[pl.BlockSpec((block, 16, cap), lambda i: (i, 0, 0)), whole(prev.shape),
                  whole(scale.shape)],
        out_specs=[whole(s) for s in shapes],
        out_shape=[jax.ShapeDtypeStruct(s, F32) for s in shapes],
        name="collect",
    )(recv, prev, scale)


def exchange(edge, strip, rows):
    groups, members = lax.axis_size("grp"), lax.axis_size("dev")

    def move(x, up, right):
        pairs = []
        for g in range(groups):
            for d in range(members):
                if 0 <= g + up < groups and 0 <= d + right < members:
                    pairs.append((g * members + d, (g + up) * members + d + right))
        return lax.ppermute(x, ("grp", "dev"), pairs)

    edges = jnp.stack([move(edge[1], 1, 0), move(edge[0], -1, 0)])
    strips = jnp.stack([move(strip[1], 0, 1), move(strip[0], 0, -1)])
    corners = jnp.stack([
        jnp.stack([move(strip[1][:, rows - SWEEPS :], 1, 1), move(strip[0][:, rows - SWEEPS :], 1, -1)]),
        jnp.stack([move(strip[1][:, :SWEEPS], -1, 1), move(strip[0][:, :SWEEPS], -1, -1)]),
    ])
    return edges, strips, corners


def sweep_kernel(rows, cols, prev_ref, load_ref, scale_ref, edge_ref, strip_ref, corner_ref,
                 inverse_ref, out_ref, one, two, base, factor):
    top = 2 * SWEEPS
    wide = cols + LANES
    tall = rows + 2 * top
    zero_rows = jnp.zeros((12, SWEEPS, wide), F32)
    for start in (0, tall - SWEEPS):
        one[:, start : start + SWEEPS, :] = zero_rows
        two[:, start : start + SWEEPS, :] = zero_rows
    one[:, top : top + rows, :cols] = prev_ref[...]
    base[:, top : top + rows, :cols] = load_ref[...]
    factor[top : top + rows, :cols] = scale_ref[...]
    for side, start in ((0, top - SWEEPS), (1, top + rows)):
        one[:, start : start + SWEEPS, :cols] = edge_ref[side, :12]
        base[:, start : start + SWEEPS, :cols] = edge_ref[side, 13:]
        factor[start : start + SWEEPS, :cols] = edge_ref[side, 12]

    def unpack(west, east, start, kind):
        size = west.shape[0]
        lane = lax.broadcasted_iota(jnp.int32, (size, LANES), 1)
        for j in range(13 if kind == 0 else 12):
            back = (LANES - j * SWEEPS) % LANES
            first = pltpu.roll(east, back, 1) if back else east
            back = (back - SWEEPS) % LANES
            last = pltpu.roll(west, back, 1) if back else west
            piece = jnp.where(lane < SWEEPS, first, jnp.where(lane >= LANES - SWEEPS, last, 0.0))
            if j == 12:
                factor[start : start + size, cols:] = piece
            elif kind == 0:
                one[j, start : start + size, cols:] = piece
            else:
                base[j, start : start + size, cols:] = piece

    for kind in range(2):
        unpack(strip_ref[0, kind], strip_ref[1, kind], top, kind)
        for side, start in ((0, top - SWEEPS), (1, top + rows)):
            unpack(corner_ref[side, 0, kind], corner_ref[side, 1, kind], start, kind)

    starts = list(range(top - SWEEPS, top + rows + SWEEPS, 8))
    for start in starts:
        here = slice(start, start + 8)
        scale = factor[here, :]
        inside = scale > 0.0
        inv = jnp.where(inside, 1.0 / jnp.where(inside, scale, 1.0), 0.0)
        loads = [base[j, here, :] for j in range(12)]
        for i in range(12):
            total = inverse_ref[i, 0] * loads[0]
            for j in range(1, 12):
                total = total + inverse_ref[i, j] * loads[j]
            base[i, here, :] = total * inv
        factor[here, :] = inv * coupling_weight

    def relax(source, target, wanted):
        for start in wanted:
            here = slice(start, start + 8)
            south = slice(start - 1, start + 7)
            north = slice(start + 1, start + 9)
            sources = []
            for node, (turn, beside, rows_at, below) in enumerate(
                ((1, 1, south, 2), (wide - 1, 0, south, 3), (1, 3, north, 0), (wide - 1, 2, north, 1))
            ):
                for c in range(3):
                    sources.append(
                        pltpu.roll(source[3 * beside + c, here, :], turn, 1)
                        + source[3 * below + c, rows_at, :]
                    )
            inv = factor[here, :]
            for i in range(12):
                total = inverse_ref[i, 0] * sources[0]
                for j in range(1, 12):
                    total = total + inverse_ref[i, j] * sources[j]
                target[i, here, :] = base[i, here, :] + total * inv

    def pair(_, carry):
        relax(one, two, starts)
        relax(two, one, starts)
        return carry

    lax.fori_loop(0, SWEEPS // 2, pair, 0)
    out_ref[...] = one[:, top : top + rows, :cols]


def sweep(rows, cols, prev, load, scale, edges, strips, corners, inverse):
    tall, wide = rows + 4 * SWEEPS, cols + LANES
    return pl.pallas_call(
        functools.partial(sweep_kernel, rows, cols),
        in_specs=[VM] * 6 + [SM],
        out_specs=VM,
        out_shape=jax.ShapeDtypeStruct((12, rows, cols), F32),
        scratch_shapes=[pltpu.VMEM((12, tall, wide), F32)] * 3 + [pltpu.VMEM((tall, wide), F32)],
        name="sweep",
    )(prev, load, scale, edges, strips, corners, inverse)


def answer_kernel(rows, cols, disp_ref, recv_ref, out_ref, table):
    @pl.when(pl.program_id(0) == 0)
    def _():
        high, low = split(disp_ref[...].reshape(12 * rows, cols))
        table[...] = jnp.concatenate([high.astype(BF16), low.astype(BF16)], axis=1)

    values = lanes_of(recv_ref)
    width = values.shape[1]
    cap = recv_ref.shape[2]
    mask = lax.broadcasted_iota(jnp.int32, (rows, width), 0).astype(F32) == values[12:13]
    low_hot = one_hot(values[13:14], cols)
    picked = jnp.dot(
        table[...], jnp.concatenate([low_hot, low_hot], axis=0), preferred_element_type=F32
    )
    lines = [
        jnp.sum(jnp.where(mask, picked[c * rows : (c + 1) * rows], 0.0), axis=0, keepdims=True)
        for c in range(12)
    ]
    result = jnp.concatenate(lines + [jnp.zeros((4, width), F32)], axis=0)
    for g in range(recv_ref.shape[0]):
        out_ref[g] = result[:, g * cap : (g + 1) * cap]


def answer(rows, cols, disp, recv):
    groups, _, cap = recv.shape
    block = max(1, min(groups, 1024 // cap))
    spec = pl.BlockSpec((block, 16, cap), lambda i: (i, 0, 0))
    return pl.pallas_call(
        functools.partial(answer_kernel, rows, cols),
        grid=(groups // block,),
        in_specs=[pl.BlockSpec(disp.shape, lambda i: (0, 0, 0)), spec],
        out_specs=spec,
        out_shape=jax.ShapeDtypeStruct(recv.shape, F32),
        scratch_shapes=[pltpu.VMEM((12 * rows, 2 * cols), BF16)],
        name="answer",
    )(disp, recv)


def finish_kernel(n, cap, back_ref, owner_ref, rank_ref, spread_ref, out_ref, table):
    @pl.when(pl.program_id(0) == 0)
    def _():
        high, low = split(back_ref[...])
        table[...] = jnp.concatenate([high.astype(BF16), low.astype(BF16)], axis=1)

    slot_hot = one_hot(rank_ref[...], cap)
    picked = jnp.dot(
        table[...], jnp.concatenate([slot_hot, slot_hot], axis=0), preferred_element_type=F32
    )
    width = owner_ref.shape[1]
    owner = jnp.broadcast_to(owner_ref[...], (16, width))
    node = jnp.zeros((16, width), F32)
    for d in range(n):
        node = jnp.where(owner == d, picked[d * 16 : (d + 1) * 16], node)
    for c in range(3):
        out_ref[c] = jnp.dot(spread_ref[c], node, precision=highest, preferred_element_type=F32)


def finish(n, cap, back, owner, rank, spread):
    faces = owner.shape[1]
    width = 512
    row = pl.BlockSpec((1, width), lambda i: (0, i))
    return pl.pallas_call(
        functools.partial(finish_kernel, n, cap),
        grid=(faces // width,),
        in_specs=[pl.BlockSpec((n * 16, cap), lambda i: (0, 0)), row, row,
                  pl.BlockSpec(spread.shape, lambda i: (0, 0, 0))],
        out_specs=pl.BlockSpec((3, NODES_F, width), lambda i: (0, 0, i)),
        out_shape=jax.ShapeDtypeStruct((3, NODES_F, faces), F32),
        scratch_shapes=[pltpu.VMEM((n * 16, 2 * cap), BF16)],
        name="finish",
    )(back, owner, rank, spread)


def swap(x):
    return lax.all_to_all(x, ("grp", "dev"), split_axis=0, concat_axis=0, tiled=True)


def local(
    face_owner,
    face_element,
    element_state,
    lift,
    face_scale,
    transfer,
    stiffness_ref,
    element_scale,
    displacement_prev,
):
    n = lax.axis_size("grp") * lax.axis_size("dev")
    faces = face_owner.shape[0]
    cap = 2 * faces // n
    rows, cols = element_scale.shape
    prev = displacement_prev.reshape(12, rows, cols)
    owner = face_owner.reshape(1, faces)
    spread = jnp.einsum("nk,cd->ncdk", transfer, jnp.eye(3, dtype=F32), precision=highest)
    spread_in = jnp.pad(spread.reshape(12, 3 * NODES_F), ((0, 4), (0, 0)))
    spread_out = jnp.pad(spread.transpose(2, 3, 0, 1).reshape(3, NODES_F, 12), ((0, 0), (0, 0), (0, 4)))
    outgoing, rank, inverse = route(
        n, cap, cols, owner, face_element.reshape(1, faces), element_state, lift,
        face_scale.reshape(1, faces), spread_in, stiffness_ref,
    )
    received = swap(outgoing.reshape(n, 16, cap))
    fold = max(1, LANES // cap)
    if fold > 1:
        received = received.reshape(n // fold, fold, 16, cap).transpose(0, 2, 1, 3)
        received = received.reshape(n // fold, 16, fold * cap)
    load, edge, strip = collect(rows, cols, received, prev, element_scale)
    edges, strips, corners = exchange(edge, strip, rows)
    disp = sweep(rows, cols, prev, load, element_scale, edges, strips, corners, inverse)
    returning = answer(rows, cols, disp, received)
    if fold > 1:
        returning = returning.reshape(n // fold, 16, fold, cap).transpose(0, 2, 1, 3)
        returning = returning.reshape(n, 16, cap)
    back = swap(returning).reshape(n * 16, cap)
    face_displacement = finish(n, cap, back, owner, rank, spread_out)
    return (disp.reshape(4, 3, rows, cols), face_displacement)


def solution(mesh):
    placed = (
        P(("grp", "dev"), None),
        P(("grp", "dev")),
        P(None, ("grp", "dev")),
        P(),
        P(("grp", "dev")),
        P(),
        P(),
        P("grp", "dev"),
        P(None, None, "grp", "dev"),
    )
    return jax.shard_map(
        local,
        mesh=mesh,
        in_specs=placed,
        out_specs=(P(None, None, "grp", "dev"), P(None, None, ("grp", "dev"))),
        check_vma=False,
    )
```

```python
import functools

import jax
import jax.numpy as jnp
from jax import lax
from jax.experimental import pallas as pl
from jax.experimental.pallas import tpu as pltpu
from jax.sharding import PartitionSpec as P

NODES_F = 10
SWEEPS = 8
LANES = 128

coupling_weight = 2.2
highest = lax.Precision.HIGHEST
F32 = jnp.float32
BF16 = jnp.bfloat16
NT = (((1,), (1,)), ((), ()))
VM = pl.BlockSpec(memory_space=pltpu.VMEM)
SM = pl.BlockSpec(memory_space=pltpu.SMEM)


def split(x):
    high = x.astype(BF16).astype(F32)
    return high, x - high


def one_hot(row, count):
    places = lax.broadcasted_iota(jnp.int32, (count, row.shape[1]), 0).astype(F32)
    return jnp.where(places == row, 1.0, 0.0).astype(BF16)


def route_kernel(n, cap, cols, owner_ref, element_ref, state_ref, lift_ref, scale_ref, spread_ref,
                 stiff_ref, out_ref, rank_ref, inverse_ref, counts):
    step = pl.program_id(0)
    width = owner_ref.shape[1]

    @pl.when(step == 0)
    def _():
        out_ref[...] = jnp.zeros_like(out_ref)
        counts[...] = jnp.zeros_like(counts)
        stiffness = stiff_ref[...]
        identity = (
            lax.broadcasted_iota(jnp.int32, (12, 12), 0)
            == lax.broadcasted_iota(jnp.int32, (12, 12), 1)
        ).astype(F32)
        approx = identity / 5.0
        for _ in range(8):
            product = jnp.dot(stiffness, approx, precision=highest, preferred_element_type=F32)
            approx = jnp.dot(
                approx, 2.0 * identity - product, precision=highest, preferred_element_type=F32
            )
        inverse_ref[...] = approx

    owner = owner_ref[...]
    owner_f = owner.astype(F32)
    traces = jnp.dot(lift_ref[...], state_ref[...], preferred_element_type=F32) * scale_ref[...]
    loads = jnp.dot(spread_ref[...], traces, precision=highest, preferred_element_type=F32)
    element = element_ref[...]
    high_row = (element // cols).astype(F32)
    low_row = (element % cols).astype(F32)
    where_row = lax.broadcasted_iota(jnp.int32, loads.shape, 0)
    values = jnp.where(where_row == 12, high_row, jnp.where(where_row == 13, low_row, loads))

    owner_hot = one_hot(owner_f, n)
    before = (
        lax.broadcasted_iota(jnp.int32, (width, width), 0)
        < lax.broadcasted_iota(jnp.int32, (width, width), 1)
    ).astype(F32).astype(BF16)
    running = jnp.dot(owner_hot, before, preferred_element_type=F32) + counts[:, :1]
    hot = owner_hot.astype(F32)
    rank = jnp.sum(hot * running, axis=0, keepdims=True)
    rank_ref[...] = rank
    counts[...] = counts[...] + jnp.sum(hot, axis=1, keepdims=True)

    slot_hot = one_hot(rank, cap)
    high, low = split(values)
    owner_wide = jnp.broadcast_to(owner, values.shape)
    highs, lows = [], []
    for d in range(n):
        mine = owner_wide == d
        highs.append(jnp.where(mine, high, 0.0).astype(BF16))
        lows.append(jnp.where(mine, low, 0.0).astype(BF16))
    left = jnp.concatenate(
        [jnp.concatenate(highs, axis=0), jnp.concatenate(lows, axis=0)], axis=1
    )
    right = jnp.concatenate([slot_hot, slot_hot], axis=1)
    out_ref[...] += lax.dot_general(left, right, NT, preferred_element_type=F32)


def route(n, cap, cols, owner, element, state, lift, scale, spread, stiffness):
    faces = owner.shape[1]
    width = 512
    whole = lambda a: pl.BlockSpec(a.shape, lambda i: (0,) * a.ndim)
    row = pl.BlockSpec((1, width), lambda i: (0, i))
    return pl.pallas_call(
        functools.partial(route_kernel, n, cap, cols),
        grid=(faces // width,),
        in_specs=[row, row, pl.BlockSpec((state.shape[0], width), lambda i: (0, i)), whole(lift),
                  row, whole(spread), whole(stiffness)],
        out_specs=[pl.BlockSpec((n * 16, cap), lambda i: (0, 0)), row,
                   pl.BlockSpec((12, 12), lambda i: (0, 0))],
        out_shape=[jax.ShapeDtypeStruct((n * 16, cap), F32),
                   jax.ShapeDtypeStruct((1, faces), F32),
                   jax.ShapeDtypeStruct((12, 12), F32)],
        scratch_shapes=[pltpu.VMEM((n, LANES), F32)],
        name="route",
    )(owner, element, state, lift, scale, spread, stiffness)


def lanes_of(ref):
    return jnp.concatenate([ref[g] for g in range(ref.shape[0])], axis=1)


def gather_kernel_in(rows, cols, recv_ref, prev_ref, scale_ref, load_ref, edge_ref, strip_ref):
    step = pl.program_id(0)

    @pl.when(step == 0)
    def _():
        load_ref[...] = jnp.zeros_like(load_ref)

    values = lanes_of(recv_ref)
    width = values.shape[1]
    mask = lax.broadcasted_iota(jnp.int32, (rows, width), 0).astype(F32) == values[12:13]
    low_hot = one_hot(values[13:14], cols)
    high, low = split(values)
    highs, lows = [], []
    for c in range(12):
        highs.append(jnp.where(mask, high[c : c + 1], 0.0).astype(BF16))
        lows.append(jnp.where(mask, low[c : c + 1], 0.0).astype(BF16))
    left = jnp.concatenate(
        [jnp.concatenate(highs, axis=0), jnp.concatenate(lows, axis=0)], axis=1
    )
    right = jnp.concatenate([low_hot, low_hot], axis=1)
    total = lax.dot_general(left, right, NT, preferred_element_type=F32)
    load_ref[...] += total.reshape(12, rows, cols)

    @pl.when(step == pl.num_programs(0) - 1)
    def _():
        scale = scale_ref[...]
        for side, start in ((0, 0), (1, rows - SWEEPS)):
            edge_ref[side, :12] = prev_ref[:, start : start + SWEEPS, :]
            edge_ref[side, 12] = scale[start : start + SWEEPS]
            edge_ref[side, 13:] = load_ref[:, start : start + SWEEPS, :]
        lane = lax.broadcasted_iota(jnp.int32, (rows, LANES), 1) // SWEEPS
        for side in range(2):
            base = 0 if side == 0 else cols - LANES
            turn = 0 if side == 0 else SWEEPS
            for kind in range(2):
                pieces = [(prev_ref if kind == 0 else load_ref)[c, :, base : base + LANES] for c in range(12)]
                if kind == 0:
                    pieces.append(scale[:, base : base + LANES])
                packed = jnp.zeros((rows, LANES), F32)
                for j, piece in enumerate(pieces):
                    move = (j * SWEEPS + turn) % LANES
                    piece = pltpu.roll(piece, move, 1) if move else piece
                    packed = jnp.where(lane == j, piece, packed)
                strip_ref[side, kind] = packed


def collect(rows, cols, recv, prev, scale):
    groups, _, cap = recv.shape
    block = max(1, min(groups, 1024 // cap))
    whole = lambda shape: pl.BlockSpec(shape, lambda i: (0,) * len(shape))
    shapes = [(12, rows, cols), (2, 25, SWEEPS, cols), (2, 2, rows, LANES)]
    return pl.pallas_call(
        functools.partial(gather_kernel_in, rows, cols),
        grid=(groups // block,),
        in_specs=[pl.BlockSpec((block, 16, cap), lambda i: (i, 0, 0)), whole(prev.shape),
                  whole(scale.shape)],
        out_specs=[whole(s) for s in shapes],
        out_shape=[jax.ShapeDtypeStruct(s, F32) for s in shapes],
        name="collect",
    )(recv, prev, scale)


MESH = pl.DeviceIdType.MESH
ANY = pl.BlockSpec(memory_space=pl.ANY)
AROUND = [(1, 0), (-1, 0), (0, 1), (0, -1), (1, 1), (1, -1), (-1, 1), (-1, -1)]


def exchange_kernel(groups, members, rows, edge, strip, edges, strips, corners, send, recv):
    g, d = lax.axis_index("grp"), lax.axis_index("dev")

    def exists(up, right):
        row, col = g + up, d + right
        return (row >= 0) & (row < groups) & (col >= 0) & (col < members)

    barrier = pltpu.get_barrier_semaphore()
    for up, right in AROUND:

        @pl.when(exists(up, right))
        def _():
            pl.semaphore_signal(barrier, inc=1, device_id=(g + up, d + right), device_id_type=MESH)

    one = lambda condition: jnp.where(condition, 1, 0).astype(jnp.int32)
    near_rows = 1 + one(g > 0) + one(g < groups - 1)
    near_cols = 1 + one(d > 0) + one(d < members - 1)
    pl.semaphore_wait(barrier, near_rows * near_cols - 1)

    copies = []
    for k, (up, right) in enumerate(AROUND):
        v, h = (0 if up == 1 else 1), (0 if right == 1 else 1)
        if right == 0:
            source, target = edge.at[1 - v], edges.at[v]
        elif up == 0:
            source, target = strip.at[1 - h], strips.at[h]
        else:
            start = rows - SWEEPS if up == 1 else 0
            source, target = strip.at[1 - h, :, pl.ds(start, SWEEPS), :], corners.at[v, h]
        copy = pltpu.make_async_remote_copy(
            src_ref=source, dst_ref=target, send_sem=send.at[k], recv_sem=recv.at[k],
            device_id=(g + up, d + right), device_id_type=MESH,
        )
        copies.append(copy)
        pl.when(exists(up, right))(copy.start)
    for k, (up, right) in enumerate(AROUND):
        pl.when(exists(up, right))(copies[k].wait_send)
        pl.when(exists(-up, -right))(copies[k].wait_recv)


def exchange(edge, strip, rows):
    groups, members = lax.axis_size("grp"), lax.axis_size("dev")
    shapes = [edge.shape, strip.shape, (2, 2, 2, SWEEPS, LANES)]
    return pl.pallas_call(
        functools.partial(exchange_kernel, groups, members, rows),
        in_specs=[ANY, ANY],
        out_specs=[ANY] * 3,
        out_shape=[jax.ShapeDtypeStruct(s, F32) for s in shapes],
        scratch_shapes=[pltpu.SemaphoreType.DMA((8,)), pltpu.SemaphoreType.DMA((8,))],
        compiler_params=pltpu.CompilerParams(collective_id=0, has_side_effects=True),
        name="exchange",
    )(edge, strip)


def swap_kernel(n, members, x, y, send, recv, own):
    me = lax.axis_index("grp") * members + lax.axis_index("dev")
    place = lambda k: lax.rem(me + k, n)
    ident = lambda t: (t // members, lax.rem(t, members))
    barrier = pltpu.get_barrier_semaphore()

    def greet(k, carry):
        pl.semaphore_signal(barrier, inc=1, device_id=ident(place(k)), device_id_type=MESH)
        return carry

    lax.fori_loop(1, n, greet, 0)
    keep = pltpu.make_async_copy(x.at[me], y.at[me], own)
    keep.start()
    pl.semaphore_wait(barrier, n - 1)

    def copy(k):
        target = place(k)
        return pltpu.make_async_remote_copy(
            src_ref=x.at[target], dst_ref=y.at[me], send_sem=send.at[k], recv_sem=recv.at[k],
            device_id=ident(target), device_id_type=MESH,
        )

    def begin(k, carry):
        copy(k).start()
        return carry

    def end(k, carry):
        copy(k).wait()
        return carry

    lax.fori_loop(1, n, begin, 0)
    keep.wait()
    lax.fori_loop(1, n, end, 0)


def swap(x, number):
    n = x.shape[0]
    return pl.pallas_call(
        functools.partial(swap_kernel, n, lax.axis_size("dev")),
        in_specs=[ANY],
        out_specs=ANY,
        out_shape=jax.ShapeDtypeStruct(x.shape, F32),
        scratch_shapes=[pltpu.SemaphoreType.DMA((n,)), pltpu.SemaphoreType.DMA((n,)),
                        pltpu.SemaphoreType.DMA],
        compiler_params=pltpu.CompilerParams(collective_id=number, has_side_effects=True),
        name=("swap_out", "swap_back")[number - 1],
    )(x)


def sweep_kernel(rows, cols, prev_ref, load_ref, scale_ref, edge_ref, strip_ref, corner_ref,
                 inverse_ref, flag_ref, out_ref, one, two, base, factor):
    top = 2 * SWEEPS
    wide = cols + LANES
    tall = rows + 2 * top
    zero_rows = jnp.zeros((12, SWEEPS, wide), F32)
    for start in (0, tall - SWEEPS):
        one[:, start : start + SWEEPS, :] = zero_rows
        two[:, start : start + SWEEPS, :] = zero_rows
    one[:, top : top + rows, :cols] = prev_ref[...]
    base[:, top : top + rows, :cols] = load_ref[...]
    factor[top : top + rows, :cols] = scale_ref[...]
    near = [flag_ref[k] > 0 for k in range(4)]
    for side, start in ((0, top - SWEEPS), (1, top + rows)):
        shell = jnp.where(near[side], edge_ref[side], 0.0)
        one[:, start : start + SWEEPS, :cols] = shell[:12]
        base[:, start : start + SWEEPS, :cols] = shell[13:]
        factor[start : start + SWEEPS, :cols] = shell[12]

    def unpack(west, east, start, kind, at_all):
        size = west.shape[0]
        west = jnp.where(near[2] & at_all, west, 0.0)
        east = jnp.where(near[3] & at_all, east, 0.0)
        lane = lax.broadcasted_iota(jnp.int32, (size, LANES), 1)
        for j in range(13 if kind == 0 else 12):
            back = (LANES - j * SWEEPS) % LANES
            first = pltpu.roll(east, back, 1) if back else east
            back = (back - SWEEPS) % LANES
            last = pltpu.roll(west, back, 1) if back else west
            piece = jnp.where(lane < SWEEPS, first, jnp.where(lane >= LANES - SWEEPS, last, 0.0))
            if j == 12:
                factor[start : start + size, cols:] = piece
            elif kind == 0:
                one[j, start : start + size, cols:] = piece
            else:
                base[j, start : start + size, cols:] = piece

    for kind in range(2):
        unpack(strip_ref[0, kind], strip_ref[1, kind], top, kind, near[2] | near[3])
        for side, start in ((0, top - SWEEPS), (1, top + rows)):
            unpack(corner_ref[side, 0, kind], corner_ref[side, 1, kind], start, kind, near[side])

    starts = list(range(top - SWEEPS, top + rows + SWEEPS, 8))
    for start in starts:
        here = slice(start, start + 8)
        scale = factor[here, :]
        inside = scale > 0.0
        inv = jnp.where(inside, 1.0 / jnp.where(inside, scale, 1.0), 0.0)
        loads = [base[j, here, :] for j in range(12)]
        for i in range(12):
            total = inverse_ref[i, 0] * loads[0]
            for j in range(1, 12):
                total = total + inverse_ref[i, j] * loads[j]
            base[i, here, :] = total * inv
        factor[here, :] = inv * coupling_weight

    def relax(source, target, wanted, offset=0):
        for start in wanted:
            here = slice(start, start + 8)
            south = slice(start - 1, start + 7)
            north = slice(start + 1, start + 9)
            sources = []
            for node, (turn, beside, rows_at, below) in enumerate(
                ((1, 1, south, 2), (wide - 1, 0, south, 3), (1, 3, north, 0), (wide - 1, 2, north, 1))
            ):
                for c in range(3):
                    sources.append(
                        pltpu.roll(source[3 * beside + c, here, :], turn, 1)
                        + source[3 * below + c, rows_at, :]
                    )
            inv = factor[here, :]
            for i in range(12):
                total = inverse_ref[i, 0] * sources[0]
                for j in range(1, 12):
                    total = total + inverse_ref[i, j] * sources[j]
                total = base[i, here, :] + total * inv
                target[i, start - offset : start - offset + 8, :] = total[:, : target.shape[2]]

    def pair(_, carry):
        relax(one, two, starts)
        relax(two, one, starts)
        return carry

    lax.fori_loop(0, SWEEPS // 2 - 1, pair, 0)
    relax(one, two, starts)
    relax(two, out_ref, starts[1:-1], top)


def sweep(rows, cols, prev, load, scale, edges, strips, corners, inverse):
    tall, wide = rows + 4 * SWEEPS, cols + LANES
    g, d = lax.axis_index("grp"), lax.axis_index("dev")
    flags = jnp.stack(
        [g > 0, g < lax.axis_size("grp") - 1, d > 0, d < lax.axis_size("dev") - 1]
    ).astype(jnp.int32)
    return pl.pallas_call(
        functools.partial(sweep_kernel, rows, cols),
        in_specs=[VM] * 6 + [SM] * 2,
        out_specs=VM,
        out_shape=jax.ShapeDtypeStruct((12, rows, cols), F32),
        scratch_shapes=[pltpu.VMEM((12, tall, wide), F32)] * 3 + [pltpu.VMEM((tall, wide), F32)],
        name="sweep",
    )(prev, load, scale, edges, strips, corners, inverse, flags)


def answer_kernel(rows, cols, disp_ref, recv_ref, out_ref, table):
    @pl.when(pl.program_id(0) == 0)
    def _():
        high, low = split(disp_ref[...].reshape(12 * rows, cols))
        table[...] = jnp.concatenate([high.astype(BF16), low.astype(BF16)], axis=1)

    values = lanes_of(recv_ref)
    width = values.shape[1]
    cap = recv_ref.shape[2]
    mask = lax.broadcasted_iota(jnp.int32, (rows, width), 0).astype(F32) == values[12:13]
    low_hot = one_hot(values[13:14], cols)
    picked = jnp.dot(
        table[...], jnp.concatenate([low_hot, low_hot], axis=0), preferred_element_type=F32
    )
    lines = [
        jnp.sum(jnp.where(mask, picked[c * rows : (c + 1) * rows], 0.0), axis=0, keepdims=True)
        for c in range(12)
    ]
    result = jnp.concatenate(lines + [jnp.zeros((4, width), F32)], axis=0)
    for g in range(recv_ref.shape[0]):
        out_ref[g] = result[:, g * cap : (g + 1) * cap]


def answer(rows, cols, disp, recv):
    groups, _, cap = recv.shape
    block = max(1, min(groups, 1024 // cap))
    spec = pl.BlockSpec((block, 16, cap), lambda i: (i, 0, 0))
    return pl.pallas_call(
        functools.partial(answer_kernel, rows, cols),
        grid=(groups // block,),
        in_specs=[pl.BlockSpec(disp.shape, lambda i: (0, 0, 0)), spec],
        out_specs=spec,
        out_shape=jax.ShapeDtypeStruct(recv.shape, F32),
        scratch_shapes=[pltpu.VMEM((12 * rows, 2 * cols), BF16)],
        name="answer",
    )(disp, recv)


def finish_kernel(n, cap, back_ref, owner_ref, rank_ref, spread_ref, out_ref, table):
    @pl.when(pl.program_id(0) == 0)
    def _():
        high, low = split(back_ref[...])
        table[...] = jnp.concatenate([high.astype(BF16), low.astype(BF16)], axis=1)

    slot_hot = one_hot(rank_ref[...], cap)
    picked = jnp.dot(
        table[...], jnp.concatenate([slot_hot, slot_hot], axis=0), preferred_element_type=F32
    )
    width = owner_ref.shape[1]
    owner = jnp.broadcast_to(owner_ref[...], (16, width))
    node = jnp.zeros((16, width), F32)
    for d in range(n):
        node = jnp.where(owner == d, picked[d * 16 : (d + 1) * 16], node)
    faced = jnp.dot(spread_ref[...], node, precision=highest, preferred_element_type=F32)
    for k in range(NODES_F):
        out_ref[k] = faced[8 * k : 8 * k + 3]


def finish(n, cap, back, owner, rank, spread):
    faces = owner.shape[1]
    width = 512
    row = pl.BlockSpec((1, width), lambda i: (0, i))
    return pl.pallas_call(
        functools.partial(finish_kernel, n, cap),
        grid=(faces // width,),
        in_specs=[pl.BlockSpec((n * 16, cap), lambda i: (0, 0)), row, row,
                  pl.BlockSpec(spread.shape, lambda i: (0, 0))],
        out_specs=pl.BlockSpec((NODES_F, 3, width), lambda i: (0, 0, i)),
        out_shape=jax.ShapeDtypeStruct((NODES_F, 3, faces), F32),
        scratch_shapes=[pltpu.VMEM((n * 16, 2 * cap), BF16)],
        name="finish",
    )(back, owner, rank, spread)


def local(
    face_owner,
    face_element,
    element_state,
    lift,
    face_scale,
    transfer,
    stiffness_ref,
    element_scale,
    displacement_prev,
):
    n = lax.axis_size("grp") * lax.axis_size("dev")
    faces = face_owner.shape[0]
    cap = 2 * faces // n
    rows, cols = element_scale.shape
    prev = displacement_prev.reshape(12, rows, cols)
    owner = face_owner.reshape(1, faces)
    spread = jnp.einsum("nk,cd->ncdk", transfer, jnp.eye(3, dtype=F32), precision=highest)
    spread_in = jnp.pad(spread.reshape(12, 3 * NODES_F), ((0, 4), (0, 0)))
    spread_out = jnp.pad(
        spread.transpose(3, 2, 0, 1).reshape(NODES_F, 3, 12), ((0, 0), (0, 5), (0, 4))
    ).reshape(8 * NODES_F, 16)
    outgoing, rank, inverse = route(
        n, cap, cols, owner, face_element.reshape(1, faces), element_state, lift,
        face_scale.reshape(1, faces), spread_in, stiffness_ref,
    )
    received = swap(outgoing.reshape(n, 16, cap), 1)
    fold = max(1, LANES // cap)
    if fold > 1:
        received = received.reshape(n // fold, fold, 16, cap).transpose(0, 2, 1, 3)
        received = received.reshape(n // fold, 16, fold * cap)
    load, edge, strip = collect(rows, cols, received, prev, element_scale)
    edges, strips, corners = exchange(edge, strip, rows)
    disp = sweep(rows, cols, prev, load, element_scale, edges, strips, corners, inverse)
    returning = answer(rows, cols, disp, received)
    if fold > 1:
        returning = returning.reshape(n // fold, 16, fold, cap).transpose(0, 2, 1, 3)
        returning = returning.reshape(n, 16, cap)
    back = swap(returning, 2).reshape(n * 16, cap)
    face_displacement = finish(n, cap, back, owner, rank, spread_out)
    return (disp.reshape(4, 3, rows, cols), face_displacement.transpose(1, 0, 2))


def solution(mesh):
    placed = (
        P(("grp", "dev"), None),
        P(("grp", "dev")),
        P(None, ("grp", "dev")),
        P(),
        P(("grp", "dev")),
        P(),
        P(),
        P("grp", "dev"),
        P(None, None, "grp", "dev"),
    )
    return jax.shard_map(
        local,
        mesh=mesh,
        in_specs=placed,
        out_specs=(P(None, None, "grp", "dev"), P(None, None, ("grp", "dev"))),
        check_vma=False,
    )
```

```python
import functools

import jax
import jax.numpy as jnp
from jax import lax
from jax.experimental import pallas as pl
from jax.experimental.pallas import tpu as pltpu
from jax.sharding import PartitionSpec as P

NODES_F = 10
SWEEPS = 8
LANES = 128

coupling_weight = 2.2
highest = lax.Precision.HIGHEST
F32 = jnp.float32
BF16 = jnp.bfloat16
NT = (((1,), (1,)), ((), ()))
VM = pl.BlockSpec(memory_space=pltpu.VMEM)
SM = pl.BlockSpec(memory_space=pltpu.SMEM)


def split(x):
    high = x.astype(BF16).astype(F32)
    return high, x - high


def one_hot(row, count):
    places = lax.broadcasted_iota(jnp.int32, (count, row.shape[1]), 0).astype(F32)
    return jnp.where(places == row, 1.0, 0.0).astype(BF16)


def route_kernel(n, cap, cols, owner_ref, element_ref, state_ref, lift_ref, scale_ref, spread_ref,
                 stiff_ref, out_ref, rank_ref, inverse_ref, counts):
    step = pl.program_id(0)
    width = owner_ref.shape[1]

    @pl.when(step == 0)
    def _():
        out_ref[...] = jnp.zeros_like(out_ref)
        counts[...] = jnp.zeros_like(counts)
        stiffness = stiff_ref[...]
        identity = (
            lax.broadcasted_iota(jnp.int32, (12, 12), 0)
            == lax.broadcasted_iota(jnp.int32, (12, 12), 1)
        ).astype(F32)
        approx = identity / 5.0
        for _ in range(8):
            product = jnp.dot(stiffness, approx, precision=highest, preferred_element_type=F32)
            approx = jnp.dot(
                approx, 2.0 * identity - product, precision=highest, preferred_element_type=F32
            )
        inverse_ref[...] = approx

    owner = owner_ref[...]
    owner_f = owner.astype(F32)
    traces = jnp.dot(lift_ref[...], state_ref[...], preferred_element_type=F32) * scale_ref[...]
    loads = jnp.dot(spread_ref[...], traces, precision=highest, preferred_element_type=F32)
    element = element_ref[...]
    high_row = (element // cols).astype(F32)
    low_row = (element % cols).astype(F32)
    where_row = lax.broadcasted_iota(jnp.int32, loads.shape, 0)
    values = jnp.where(where_row == 12, high_row, jnp.where(where_row == 13, low_row, loads))

    owner_hot = one_hot(owner_f, n)
    before = (
        lax.broadcasted_iota(jnp.int32, (width, width), 0)
        < lax.broadcasted_iota(jnp.int32, (width, width), 1)
    ).astype(F32).astype(BF16)
    running = jnp.dot(owner_hot, before, preferred_element_type=F32) + counts[:, :1]
    hot = owner_hot.astype(F32)
    rank = jnp.sum(hot * running, axis=0, keepdims=True)
    rank_ref[...] = rank
    counts[...] = counts[...] + jnp.sum(hot, axis=1, keepdims=True)

    slot_hot = one_hot(rank, cap)
    high, low = split(values)
    owner_wide = jnp.broadcast_to(owner, values.shape)
    highs, lows = [], []
    for d in range(n):
        mine = owner_wide == d
        highs.append(jnp.where(mine, high, 0.0).astype(BF16))
        lows.append(jnp.where(mine, low, 0.0).astype(BF16))
    left = jnp.concatenate(
        [jnp.concatenate(highs, axis=0), jnp.concatenate(lows, axis=0)], axis=1
    )
    right = jnp.concatenate([slot_hot, slot_hot], axis=1)
    out_ref[...] += lax.dot_general(left, right, NT, preferred_element_type=F32)


def route(n, cap, cols, owner, element, state, lift, scale, spread, stiffness):
    faces = owner.shape[1]
    width = 512
    whole = lambda a: pl.BlockSpec(a.shape, lambda i: (0,) * a.ndim)
    row = pl.BlockSpec((1, width), lambda i: (0, i))
    return pl.pallas_call(
        functools.partial(route_kernel, n, cap, cols),
        grid=(faces // width,),
        in_specs=[row, row, pl.BlockSpec((state.shape[0], width), lambda i: (0, i)), whole(lift),
                  row, whole(spread), whole(stiffness)],
        out_specs=[pl.BlockSpec((n * 16, cap), lambda i: (0, 0)), row,
                   pl.BlockSpec((12, 12), lambda i: (0, 0))],
        out_shape=[jax.ShapeDtypeStruct((n * 16, cap), F32),
                   jax.ShapeDtypeStruct((1, faces), F32),
                   jax.ShapeDtypeStruct((12, 12), F32)],
        scratch_shapes=[pltpu.VMEM((n, LANES), F32)],
        name="route",
    )(owner, element, state, lift, scale, spread, stiffness)


def lanes_of(ref):
    return jnp.concatenate([ref[g] for g in range(ref.shape[0])], axis=1)


def gather_kernel_in(rows, cols, recv_ref, prev_ref, scale_ref, load_ref, edge_ref, strip_ref):
    step = pl.program_id(0)

    @pl.when(step == 0)
    def _():
        load_ref[...] = jnp.zeros_like(load_ref)

    values = lanes_of(recv_ref)
    width = values.shape[1]
    mask = lax.broadcasted_iota(jnp.int32, (rows, width), 0).astype(F32) == values[12:13]
    low_hot = one_hot(values[13:14], cols)
    high, low = split(values)
    highs, lows = [], []
    for c in range(12):
        highs.append(jnp.where(mask, high[c : c + 1], 0.0).astype(BF16))
        lows.append(jnp.where(mask, low[c : c + 1], 0.0).astype(BF16))
    left = jnp.concatenate(
        [jnp.concatenate(highs, axis=0), jnp.concatenate(lows, axis=0)], axis=1
    )
    right = jnp.concatenate([low_hot, low_hot], axis=1)
    total = lax.dot_general(left, right, NT, preferred_element_type=F32)
    load_ref[...] += total.reshape(12, rows, cols)

    @pl.when(step == pl.num_programs(0) - 1)
    def _():
        scale = scale_ref[...]
        for side, start in ((0, 0), (1, rows - SWEEPS)):
            edge_ref[side, :12] = prev_ref[:, start : start + SWEEPS, :]
            edge_ref[side, 12] = scale[start : start + SWEEPS]
            edge_ref[side, 13:] = load_ref[:, start : start + SWEEPS, :]
        lane = lax.broadcasted_iota(jnp.int32, (rows, LANES), 1) // SWEEPS
        for side in range(2):
            base = 0 if side == 0 else cols - LANES
            turn = 0 if side == 0 else SWEEPS
            for kind in range(2):
                pieces = [(prev_ref if kind == 0 else load_ref)[c, :, base : base + LANES] for c in range(12)]
                if kind == 0:
                    pieces.append(scale[:, base : base + LANES])
                packed = jnp.zeros((rows, LANES), F32)
                for j, piece in enumerate(pieces):
                    move = (j * SWEEPS + turn) % LANES
                    piece = pltpu.roll(piece, move, 1) if move else piece
                    packed = jnp.where(lane == j, piece, packed)
                strip_ref[side, kind] = packed


def collect(rows, cols, recv, prev, scale):
    groups, _, cap = recv.shape
    block = max(1, min(groups, 1024 // cap))
    whole = lambda shape: pl.BlockSpec(shape, lambda i: (0,) * len(shape))
    shapes = [(12, rows, cols), (2, 25, SWEEPS, cols), (2, 2, rows, LANES)]
    return pl.pallas_call(
        functools.partial(gather_kernel_in, rows, cols),
        grid=(groups // block,),
        in_specs=[pl.BlockSpec((block, 16, cap), lambda i: (i, 0, 0)), whole(prev.shape),
                  whole(scale.shape)],
        out_specs=[whole(s) for s in shapes],
        out_shape=[jax.ShapeDtypeStruct(s, F32) for s in shapes],
        name="collect",
    )(recv, prev, scale)


MESH = pl.DeviceIdType.MESH
ANY = pl.BlockSpec(memory_space=pl.ANY)
AROUND = [(1, 0), (-1, 0), (0, 1), (0, -1), (1, 1), (1, -1), (-1, 1), (-1, -1)]


def exchange_kernel(groups, members, rows, edge, strip, edges, strips, corners, send, recv):
    g, d = lax.axis_index("grp"), lax.axis_index("dev")

    def exists(up, right):
        row, col = g + up, d + right
        return (row >= 0) & (row < groups) & (col >= 0) & (col < members)

    barrier = pltpu.get_barrier_semaphore()
    for up, right in AROUND:

        @pl.when(exists(up, right))
        def _():
            pl.semaphore_signal(barrier, inc=1, device_id=(g + up, d + right), device_id_type=MESH)

    one = lambda condition: jnp.where(condition, 1, 0).astype(jnp.int32)
    near_rows = 1 + one(g > 0) + one(g < groups - 1)
    near_cols = 1 + one(d > 0) + one(d < members - 1)
    pl.semaphore_wait(barrier, near_rows * near_cols - 1)

    copies = []
    for k, (up, right) in enumerate(AROUND):
        v, h = (0 if up == 1 else 1), (0 if right == 1 else 1)
        if right == 0:
            source, target = edge.at[1 - v], edges.at[v]
        elif up == 0:
            source, target = strip.at[1 - h], strips.at[h]
        else:
            start = rows - SWEEPS if up == 1 else 0
            source, target = strip.at[1 - h, :, pl.ds(start, SWEEPS), :], corners.at[v, h]
        copy = pltpu.make_async_remote_copy(
            src_ref=source, dst_ref=target, send_sem=send.at[k], recv_sem=recv.at[k],
            device_id=(g + up, d + right), device_id_type=MESH,
        )
        copies.append(copy)
        pl.when(exists(up, right))(copy.start)
    for k, (up, right) in enumerate(AROUND):
        pl.when(exists(up, right))(copies[k].wait_send)
        pl.when(exists(-up, -right))(copies[k].wait_recv)


def exchange(edge, strip, rows):
    groups, members = lax.axis_size("grp"), lax.axis_size("dev")
    shapes = [edge.shape, strip.shape, (2, 2, 2, SWEEPS, LANES)]
    return pl.pallas_call(
        functools.partial(exchange_kernel, groups, members, rows),
        in_specs=[ANY, ANY],
        out_specs=[ANY] * 3,
        out_shape=[jax.ShapeDtypeStruct(s, F32) for s in shapes],
        scratch_shapes=[pltpu.SemaphoreType.DMA((8,)), pltpu.SemaphoreType.DMA((8,))],
        compiler_params=pltpu.CompilerParams(collective_id=0, has_side_effects=True),
        name="exchange",
    )(edge, strip)


def swap_kernel(n, members, x, y, send, recv, own):
    me = lax.axis_index("grp") * members + lax.axis_index("dev")
    place = lambda k: lax.rem(me + k, n)
    ident = lambda t: (t // members, lax.rem(t, members))
    barrier = pltpu.get_barrier_semaphore()

    def greet(k, carry):
        pl.semaphore_signal(barrier, inc=1, device_id=ident(place(k)), device_id_type=MESH)
        return carry

    lax.fori_loop(1, n, greet, 0)
    keep = pltpu.make_async_copy(x.at[me], y.at[me], own)
    keep.start()
    pl.semaphore_wait(barrier, n - 1)

    def copy(k):
        target = place(k)
        return pltpu.make_async_remote_copy(
            src_ref=x.at[target], dst_ref=y.at[me], send_sem=send.at[k], recv_sem=recv.at[k],
            device_id=ident(target), device_id_type=MESH,
        )

    def begin(k, carry):
        copy(k).start()
        return carry

    def end(k, carry):
        copy(k).wait()
        return carry

    lax.fori_loop(1, n, begin, 0)
    keep.wait()
    lax.fori_loop(1, n, end, 0)


def swap(x, number):
    n = x.shape[0]
    return pl.pallas_call(
        functools.partial(swap_kernel, n, lax.axis_size("dev")),
        in_specs=[ANY],
        out_specs=ANY,
        out_shape=jax.ShapeDtypeStruct(x.shape, F32),
        scratch_shapes=[pltpu.SemaphoreType.DMA((n,)), pltpu.SemaphoreType.DMA((n,)),
                        pltpu.SemaphoreType.DMA],
        compiler_params=pltpu.CompilerParams(collective_id=number, has_side_effects=True),
        name=("swap_out", "swap_back")[number - 1],
    )(x)


def sweep_kernel(rows, cols, prev_ref, load_ref, scale_ref, edge_ref, strip_ref, corner_ref,
                 inverse_ref, flag_ref, out_ref, one, two, base, factor):
    top = 2 * SWEEPS
    wide = cols + LANES
    tall = rows + 2 * top
    zero_rows = jnp.zeros((12, SWEEPS, wide), F32)
    for start in (0, tall - SWEEPS):
        one[:, start : start + SWEEPS, :] = zero_rows
        two[:, start : start + SWEEPS, :] = zero_rows
    one[:, top : top + rows, :cols] = prev_ref[...]
    base[:, top : top + rows, :cols] = load_ref[...]
    factor[top : top + rows, :cols] = scale_ref[...]
    near = [flag_ref[k] > 0 for k in range(4)]
    for side, start in ((0, top - SWEEPS), (1, top + rows)):
        shell = jnp.where(near[side], edge_ref[side], 0.0)
        one[:, start : start + SWEEPS, :cols] = shell[:12]
        base[:, start : start + SWEEPS, :cols] = shell[13:]
        factor[start : start + SWEEPS, :cols] = shell[12]

    def unpack(west, east, start, kind, at_all):
        size = west.shape[0]
        west = jnp.where(near[2] & at_all, west, 0.0)
        east = jnp.where(near[3] & at_all, east, 0.0)
        lane = lax.broadcasted_iota(jnp.int32, (size, LANES), 1)
        for j in range(13 if kind == 0 else 12):
            back = (LANES - j * SWEEPS) % LANES
            first = pltpu.roll(east, back, 1) if back else east
            back = (back - SWEEPS) % LANES
            last = pltpu.roll(west, back, 1) if back else west
            piece = jnp.where(lane < SWEEPS, first, jnp.where(lane >= LANES - SWEEPS, last, 0.0))
            if j == 12:
                factor[start : start + size, cols:] = piece
            elif kind == 0:
                one[j, start : start + size, cols:] = piece
            else:
                base[j, start : start + size, cols:] = piece

    for kind in range(2):
        unpack(strip_ref[0, kind], strip_ref[1, kind], top, kind, near[2] | near[3])
        for side, start in ((0, top - SWEEPS), (1, top + rows)):
            unpack(corner_ref[side, 0, kind], corner_ref[side, 1, kind], start, kind, near[side])

    starts = list(range(top - SWEEPS, top + rows + SWEEPS, 8))
    for start in starts:
        here = slice(start, start + 8)
        scale = factor[here, :]
        inside = scale > 0.0
        inv = jnp.where(inside, 1.0 / jnp.where(inside, scale, 1.0), 0.0)
        loads = [base[j, here, :] for j in range(12)]
        for i in range(12):
            total = inverse_ref[i, 0] * loads[0]
            for j in range(1, 12):
                total = total + inverse_ref[i, j] * loads[j]
            base[i, here, :] = total * inv
        factor[here, :] = inv * coupling_weight

    def relax(source, target, wanted, offset=0):
        for start in wanted:
            here = slice(start, start + 8)
            south = slice(start - 1, start + 7)
            north = slice(start + 1, start + 9)
            sources = []
            for node, (turn, beside, rows_at, below) in enumerate(
                ((1, 1, south, 2), (wide - 1, 0, south, 3), (1, 3, north, 0), (wide - 1, 2, north, 1))
            ):
                for c in range(3):
                    sources.append(
                        pltpu.roll(source[3 * beside + c, here, :], turn, 1)
                        + source[3 * below + c, rows_at, :]
                    )
            inv = factor[here, :]
            for i in range(12):
                total = inverse_ref[i, 0] * sources[0]
                for j in range(1, 12):
                    total = total + inverse_ref[i, j] * sources[j]
                total = base[i, here, :] + total * inv
                target[i, start - offset : start - offset + 8, :] = total[:, : target.shape[2]]

    def pair(_, carry):
        relax(one, two, starts)
        relax(two, one, starts)
        return carry

    lax.fori_loop(0, SWEEPS // 2 - 1, pair, 0)
    relax(one, two, starts)
    relax(two, out_ref, starts[1:-1], top)


def sweep(rows, cols, prev, load, scale, edges, strips, corners, inverse):
    tall, wide = rows + 4 * SWEEPS, cols + LANES
    g, d = lax.axis_index("grp"), lax.axis_index("dev")
    flags = jnp.stack(
        [g > 0, g < lax.axis_size("grp") - 1, d > 0, d < lax.axis_size("dev") - 1]
    ).astype(jnp.int32)
    return pl.pallas_call(
        functools.partial(sweep_kernel, rows, cols),
        in_specs=[VM] * 6 + [SM] * 2,
        out_specs=VM,
        out_shape=jax.ShapeDtypeStruct((12, rows, cols), F32),
        scratch_shapes=[pltpu.VMEM((12, tall, wide), F32)] * 3 + [pltpu.VMEM((tall, wide), F32)],
        name="sweep",
    )(prev, load, scale, edges, strips, corners, inverse, flags)


def shape_back(cap):
    halves = max(1, cap // LANES)
    return halves, -(-12 * halves // 8) * 8


def answer_kernel(rows, cols, disp_ref, recv_ref, out_ref, table):
    @pl.when(pl.program_id(0) == 0)
    def _():
        high, low = split(disp_ref[...].reshape(12 * rows, cols))
        table[...] = jnp.concatenate([high.astype(BF16), low.astype(BF16)], axis=1)

    values = lanes_of(recv_ref)
    width = values.shape[1]
    cap = recv_ref.shape[2]
    mask = lax.broadcasted_iota(jnp.int32, (rows, width), 0).astype(F32) == values[12:13]
    low_hot = one_hot(values[13:14], cols)
    picked = jnp.dot(
        table[...], jnp.concatenate([low_hot, low_hot], axis=0), preferred_element_type=F32
    )
    lines = [
        jnp.sum(jnp.where(mask, picked[c * rows : (c + 1) * rows], 0.0), axis=0, keepdims=True)
        for c in range(12)
    ]
    halves, deep = shape_back(cap)
    lanes = cap // halves
    result = jnp.concatenate(lines, axis=0)
    pad = [jnp.zeros((deep - 12 * halves, lanes), F32)] if deep > 12 * halves else []
    for g in range(recv_ref.shape[0]):
        parts = [
            result[:, g * cap + h * lanes : g * cap + (h + 1) * lanes] for h in range(halves)
        ]
        out_ref[g] = jnp.concatenate(parts + pad, axis=0)


def answer(rows, cols, disp, recv):
    groups, _, cap = recv.shape
    block = max(1, min(groups, 1024 // cap))
    halves, deep = shape_back(cap)
    spec = pl.BlockSpec((block, 16, cap), lambda i: (i, 0, 0))
    return pl.pallas_call(
        functools.partial(answer_kernel, rows, cols),
        grid=(groups // block,),
        in_specs=[pl.BlockSpec(disp.shape, lambda i: (0, 0, 0)), spec],
        out_specs=pl.BlockSpec((block, deep, cap // halves), lambda i: (i, 0, 0)),
        out_shape=jax.ShapeDtypeStruct((groups, deep, cap // halves), F32),
        scratch_shapes=[pltpu.VMEM((12 * rows, 2 * cols), BF16)],
        name="answer",
    )(disp, recv)


def finish_kernel(n, cap, back_ref, owner_ref, rank_ref, spread_ref, out_ref, table):
    @pl.when(pl.program_id(0) == 0)
    def _():
        high, low = split(back_ref[...])
        table[...] = jnp.concatenate([high.astype(BF16), low.astype(BF16)], axis=1)

    halves, deep = shape_back(cap)
    lanes = cap // halves
    rank = rank_ref[...].astype(jnp.int32)
    part = rank // lanes
    slot_hot = one_hot((rank - part * lanes).astype(F32), lanes)
    picked = jnp.dot(
        table[...], jnp.concatenate([slot_hot, slot_hot], axis=0), preferred_element_type=F32
    )
    width = owner_ref.shape[1]
    owner = jnp.broadcast_to(owner_ref[...], (deep, width))
    found = jnp.zeros((deep, width), F32)
    for d in range(n):
        found = jnp.where(owner == d, picked[d * deep : (d + 1) * deep], found)
    node = found[:12]
    for h in range(1, halves):
        node = jnp.where(part == h, found[12 * h : 12 * h + 12], node)
    faced = jnp.dot(spread_ref[...], node, precision=highest, preferred_element_type=F32)
    for k in range(NODES_F):
        out_ref[k] = faced[8 * k : 8 * k + 3]


def finish(n, cap, back, owner, rank, spread):
    faces = owner.shape[1]
    width = 512
    row = pl.BlockSpec((1, width), lambda i: (0, i))
    return pl.pallas_call(
        functools.partial(finish_kernel, n, cap),
        grid=(faces // width,),
        in_specs=[pl.BlockSpec(back.shape, lambda i: (0, 0)), row, row,
                  pl.BlockSpec(spread.shape, lambda i: (0, 0))],
        out_specs=pl.BlockSpec((NODES_F, 3, width), lambda i: (0, 0, i)),
        out_shape=jax.ShapeDtypeStruct((NODES_F, 3, faces), F32),
        scratch_shapes=[pltpu.VMEM((back.shape[0], 2 * back.shape[1]), BF16)],
        name="finish",
    )(back, owner, rank, spread)


def local(
    face_owner,
    face_element,
    element_state,
    lift,
    face_scale,
    transfer,
    stiffness_ref,
    element_scale,
    displacement_prev,
):
    n = lax.axis_size("grp") * lax.axis_size("dev")
    faces = face_owner.shape[0]
    cap = 2 * faces // n
    rows, cols = element_scale.shape
    prev = displacement_prev.reshape(12, rows, cols)
    owner = face_owner.reshape(1, faces)
    spread = jnp.einsum("nk,cd->ncdk", transfer, jnp.eye(3, dtype=F32), precision=highest)
    spread_in = jnp.pad(spread.reshape(12, 3 * NODES_F), ((0, 4), (0, 0)))
    spread_out = jnp.pad(
        spread.transpose(3, 2, 0, 1).reshape(NODES_F, 3, 12), ((0, 0), (0, 5), (0, 0))
    ).reshape(8 * NODES_F, 12)
    outgoing, rank, inverse = route(
        n, cap, cols, owner, face_element.reshape(1, faces), element_state, lift,
        face_scale.reshape(1, faces), spread_in, stiffness_ref,
    )
    received = swap(outgoing.reshape(n, 16, cap), 1)
    fold = max(1, LANES // cap)
    if fold > 1:
        received = received.reshape(n // fold, fold, 16, cap).transpose(0, 2, 1, 3)
        received = received.reshape(n // fold, 16, fold * cap)
    load, edge, strip = collect(rows, cols, received, prev, element_scale)
    edges, strips, corners = exchange(edge, strip, rows)
    disp = sweep(rows, cols, prev, load, element_scale, edges, strips, corners, inverse)
    returning = answer(rows, cols, disp, received)
    if fold > 1:
        returning = returning.reshape(n // fold, 16, fold, cap).transpose(0, 2, 1, 3)
        returning = returning.reshape(n, 16, cap)
    back = swap(returning, 2)
    back = back.reshape(-1, back.shape[2])
    face_displacement = finish(n, cap, back, owner, rank, spread_out)
    return (disp.reshape(4, 3, rows, cols), face_displacement.transpose(1, 0, 2))


def solution(mesh):
    placed = (
        P(("grp", "dev"), None),
        P(("grp", "dev")),
        P(None, ("grp", "dev")),
        P(),
        P(("grp", "dev")),
        P(),
        P(),
        P("grp", "dev"),
        P(None, None, "grp", "dev"),
    )
    return jax.shard_map(
        local,
        mesh=mesh,
        in_specs=placed,
        out_specs=(P(None, None, "grp", "dev"), P(None, None, ("grp", "dev"))),
        check_vma=False,
    )
```
